512 devices in a mesh: rep: 32 (over x, y, z_hi), tp: 16 (over z_lo, core).
Axes of the slice: x: 4, y: 4, z: 16 (z_hi: 2, z_lo: 8; z = z_hi * 8 + z_lo), core: 2. Of those that a mesh axis runs over, the one named last changes fastest.
Arguments:
- context: bfloat16 [32, 3, 512, 2560], P('rep', None, 'tp'), may hold values from -6 to 6
- residual: bfloat16 [32, 3, 2560, 512], P('rep', None, 'tp'), may hold values from -6 to 6
- cotangent: bfloat16 [32, 3, 2560, 512], P('rep', None, 'tp'), may hold values from -6 to 6
- norm_gain: bfloat16 [2560], P('tp'), may hold values from 0.099609375 to 1.8984375
- weight: bfloat16 [32, 2560, 2560], P('rep', 'tp'), may hold values from -6 to 6
- momentum: bfloat16 [32, 2560, 2560], P('rep', 'tp'), may hold values from -4 to 4
- round_start: int32 [1], replicated, may hold values from 0 to 31
Outputs:
- weight_out: bfloat16 [32, 2560, 2560], P('rep', 'tp')
- momentum_out: bfloat16 [32, 2560, 2560], P('rep', 'tp')
The draws below stay inside these ranges and needn't reach their ends.
Inputs may be any that keep to these rules, and one draw needn't show every extreme that they name: Step s of the window averages with the replica whose index differs in bit number (round_start + s) mod log2(32).
All inputs are finite; a program needn't handle non-finite values.
Results may differ from the reference program's by a relative error of at most 0.015.
Values may be sent and summed in bfloat16 or wider, within the bound.
A program may use at most 64 MiB of HBM per device.

```python
import jax
import jax.numpy as jnp
from jax import lax

D = 2560
HF = 2560
SEQ = 512
STEPS = 3
REPLICAS = 32
N_REP = 32


def levels(stream_key, extent, shards, smallest, top_value):
    factor_of = 1.0
    for axis_at, blocks in shards:
        heights = jax.random.uniform(jax.random.fold_in(jax.random.fold_in(stream_key, 6), axis_at), (blocks,), jnp.float32, smallest / len(shards), top_value / len(shards))
        factor_of = factor_of * jnp.repeat(jnp.exp(heights), extent[axis_at] // blocks).reshape((-1,) + (1,) * (len(extent) - 1 - axis_at))
    return factor_of


def gaussian(stream_key, shape, deviation, most, split=(), held_as=jnp.bfloat16):
    values = deviation * jax.random.normal(stream_key, shape, jnp.float32)
    if split:
        values = values * levels(stream_key, shape, split, -0.22, 0.18)
    return jnp.clip(values, -most, most).astype(held_as)


def setup_inputs(seed: int = 0) -> dict:
    streams_of = jax.random.split(jax.random.key(seed), 8)
    context = gaussian(streams_of[0], (REPLICAS, STEPS, SEQ, HF), 1.0, 6.0, ((0, 32), (2, 16)))
    residual = gaussian(streams_of[1], (REPLICAS, STEPS, D, SEQ), 1.0, 6.0, ((0, 32), (2, 16)))
    cotangent = gaussian(streams_of[2], (REPLICAS, STEPS, D, SEQ), 1.0, 6.0, ((0, 32), (2, 16)))
    norm_gain = jnp.clip(1.0 + 0.18 * jax.random.normal(streams_of[3], (D,), jnp.float32), 0.099609375, 1.8984375).astype(jnp.bfloat16)
    weight = gaussian(streams_of[4], (REPLICAS, D, HF), 1.0, 6.0, ((0, 32), (1, 16)))
    momentum = gaussian(streams_of[5], (REPLICAS, D, HF), 0.5, 4.0, ((0, 32), (1, 16)))
    round_start = jax.random.randint(streams_of[6], (1,), 0, N_REP).astype(jnp.int32)
    return {"context": context, "residual": residual, "cotangent": cotangent, "norm_gain": norm_gain, "weight": weight, "momentum": momentum, "round_start": round_start}


learn_rate = 0.5
beta_decay = 0.9
epsilon = 1e-05

def replica_update(operands):
    weight_now, moment_now, context_now, residual_now, cotangent_now, gain_now = operands
    out_scale = HF ** (-0.5)
    projected = jnp.dot(weight_now, context_now.T, preferred_element_type=jnp.float32) * out_scale
    hidden = residual_now.astype(jnp.float32) + projected
    inverse = lax.rsqrt(lax.optimization_barrier(jnp.mean(hidden * hidden, axis=0, keepdims=True)) + epsilon)
    weighted = cotangent_now.astype(jnp.float32) * gain_now.astype(jnp.float32)[:, None]
    cross_mean = lax.optimization_barrier(jnp.mean(weighted * hidden, axis=0, keepdims=True))
    grad_hidden = (inverse * weighted - hidden * inverse * inverse * inverse * cross_mean).astype(jnp.bfloat16)
    gradient = jnp.dot(grad_hidden, context_now, preferred_element_type=jnp.float32) * out_scale
    fresh_moment = (beta_decay * moment_now.astype(jnp.float32) + gradient).astype(jnp.bfloat16)
    fresh_weight = (weight_now.astype(jnp.float32) - learn_rate * fresh_moment.astype(jnp.float32)).astype(jnp.bfloat16)
    return (fresh_weight, fresh_moment)

def reference(context, residual, cotangent, norm_gain, weight, momentum, round_start):
    bit_count = N_REP.bit_length() - 1
    gains = jnp.broadcast_to(norm_gain, (N_REP, D))
    for section in range(STEPS):
        weight, momentum = lax.map(replica_update, (weight, momentum, context[:, section], residual[:, section], cotangent[:, section], gains))
        bit_pick = ((round_start[0] + section) % bit_count).astype(jnp.int32)
        partner = jnp.bitwise_xor(jnp.arange(N_REP, dtype=jnp.int32), jnp.left_shift(jnp.ones((), jnp.int32), bit_pick))
        weight = ((weight.astype(jnp.float32) + weight[partner].astype(jnp.float32)) * 0.5).astype(jnp.bfloat16)
        momentum = ((momentum.astype(jnp.float32) + momentum[partner].astype(jnp.float32)) * 0.5).astype(jnp.bfloat16)
    return (weight, momentum)
```

```python
import functools

import jax
import jax.numpy as jnp
from jax import lax
from jax.experimental import pallas as pl
from jax.experimental.pallas import tpu as pltpu
from jax.sharding import PartitionSpec as P

D = 2560
HF = 2560
SEQ = 512
STEPS = 3
TP = 16
ROWS = D // TP
TOK = SEQ // TP
WIDE = 512
CH = HF // WIDE
ROUNDS = 7
HALF = TOK // 2
LEARN = 0.5
DECAY = 0.9
EPS = 1e-05
SCALE = HF**-0.5
MESH = pl.DeviceIdType.MESH
BF = jnp.bfloat16
F32 = jnp.float32


def kernel(
    bits,
    ctx,
    res,
    cot,
    gain,
    weight,
    moment,
    w_out,
    m_out,
    G,
    WB,
    MB,
    FM,
    RW,
    RM,
    resb,
    cotb,
    HID,
    SB,
    ring_r,
    ring_s,
    sib_r,
    sib_s,
    loc,
    fm_r,
    fm_s,
    w_r,
    w_s,
    sum_r,
    sum_s,
    outs,
):
    rep = lax.axis_index("rep")
    tp = lax.axis_index("tp")
    core = tp % 2
    z_hi = rep % 2
    z = z_hi * 8 + tp // 2
    base = rep - z_hi

    def at_z(place):
        return (base + place // 8, (place % 8) * 2 + core)

    up_z, down_z = (z + 1) % 16, (z + 15) % 16
    up, down = at_z(up_z), at_z(down_z)
    sibling = (rep, tp + 1 - 2 * core)

    def peer_of(bit):
        d = 1 << bit
        return (rep + d - 2 * d * ((rep // d) % 2), tp)

    peers = [peer_of(b) for b in bits]

    def remote(src, dst, send, recv, device):
        return pltpu.make_async_remote_copy(
            src_ref=src, dst_ref=dst, send_sem=send, recv_sem=recv, device_id=device, device_id_type=MESH
        )

    loads = []
    for j in range(CH):
        cols = pl.ds(WIDE * j, WIDE)
        loads.append(pltpu.make_async_copy(weight.at[0, :, cols], WB.at[0, j], loc.at[j]))
        loads.append(pltpu.make_async_copy(moment.at[0, :, cols], MB.at[0, j], loc.at[CH + j]))
    loads.append(pltpu.make_async_copy(res.at[0], resb, loc.at[2 * CH]))
    loads.append(pltpu.make_async_copy(cot.at[0], cotb, loc.at[2 * CH + 1]))
    for s in range(STEPS):
        loads.append(pltpu.make_async_copy(ctx.at[0, s], G.at[s, tp], loc.at[2 * CH + 2 + s]))
    for c in loads:
        c.start()

    barrier = pltpu.get_barrier_semaphore()
    greet = [(rep, (tp + j) % TP) for j in range(1, TP)] + [up, down] + peers
    for d in greet:
        pl.semaphore_signal(barrier, inc=1, device_id=d, device_id_type=MESH)
    pl.semaphore_wait(barrier, len(greet))

    def slot(origin, receiver_z):
        return ((origin // 8 + receiver_z // 8) % 2) * 16 + (origin % 8) * 2 + core

    def ring(s, way, k, h):
        origin = (z + 16 - (k - 1)) % 16 if way == 0 else (z + (k - 1)) % 16
        target, target_z = (up, up_z) if way == 0 else (down, down_z)
        rows = pl.ds(HALF * h, HALF)
        src = ctx.at[0, s, rows] if k == 1 else G.at[s, slot(origin, z), rows]
        return remote(
            src, G.at[s, slot(origin, target_z), rows], ring_s.at[s], ring_r.at[s, way, k - 1, h], target
        )

    def to_sibling(s, way, k):
        origin = (z + 16 - k) % 16 if way == 0 else (z + k) % 16
        place = slot(origin, z)
        return remote(G.at[s, place], G.at[s, place], sib_s.at[s], sib_r.at[s], sibling)

    def pumps():
        for s in range(STEPS):
            for k in range(1, ROUNDS + 1):
                for h in (0, 1):
                    for way in (0, 1):
                        if k > 1:
                            ring(s, way, k - 1, h).wait_recv()
                        ring(s, way, k, h).start()
                    if k > 1 and h == 1:
                        for way in (0, 1):
                            to_sibling(s, way, k - 1).start()
                    if k == 1 and h == 1:
                        remote(ctx.at[0, s], G.at[s, tp], sib_s.at[s], sib_r.at[s], sibling).start()
                    if k == ROUNDS and s + 1 < STEPS:
                        pass
                    yield s
            for h in (0, 1):
                for way in (0, 1):
                    ring(s, way, ROUNDS, h).wait_recv()
            for way in (0, 1):
                to_sibling(s, way, ROUNDS).start()
            yield s

    state = {"gen": pumps(), "count": 0}
    PER = 2 * ROUNDS + 1

    def pump(n=1):
        for _ in range(n):
            if state["count"] < PER * STEPS:
                next(state["gen"])
                state["count"] += 1

    def gathered(s):
        while state["count"] < PER * (s + 1):
            pump()
        whole = G.at[s, pl.ds(0, 15)]
        remote(whole, whole, sib_s.at[s], sib_r.at[s], sibling).wait_recv()

    def context_block(s, j):
        return G[s, 0:16, :, WIDE * j : WIDE * (j + 1)].reshape(SEQ, WIDE)

    def fm_copy(s, j):
        return remote(FM.at[s, j], RM.at[s, j], fm_s.at[s], fm_r.at[s, j], peers[s])

    def w_copy(s, j):
        src = weight.at[0, :, pl.ds(WIDE * j, WIDE)] if s == 0 else WB.at[s, j]
        return remote(src, RW.at[s, j], w_s.at[s], w_r.at[s, j], peers[s])

    def project(s, j):
        part = lax.dot_general(
            WB[s, j], context_block(s, j), (((1,), (1,)), ((), ())), preferred_element_type=F32
        )
        if j == 0:
            HID[...] = part
        else:
            HID[...] += part

    pump(2)
    for j in range(CH):
        w_copy(0, j).start()
    for c in loads:
        c.wait()
    gathered(0)
    pump(2)
    for j in range(CH):
        project(0, j)
        if j % 2:
            pump()

    for s in range(STEPS):
        hidden = HID[...] * SCALE + resb[s].astype(F32)
        HID[...] = hidden
        weighted = cotb[s].astype(F32) * gain[...]
        squares = jnp.sum(hidden * hidden, axis=0, keepdims=True)
        crosses = jnp.sum(weighted * hidden, axis=0, keepdims=True)
        SB[s, TP - 1] = jnp.concatenate(
            [v[:, 128 * a : 128 * (a + 1)] for v in (squares, crosses) for a in range(4)], axis=0
        )
        for j in range(1, TP):
            remote(
                SB.at[s, TP - 1], SB.at[s, j - 1], sum_s.at[s], sum_r.at[s], (rep, (tp + j) % TP)
            ).start()
        pump(4)
        others = SB.at[s, pl.ds(0, TP - 1)]
        remote(others, others, sum_s.at[s], sum_r.at[s], sibling).wait_recv()
        total = jnp.sum(SB[s], axis=0)
        square_sum = jnp.concatenate([total[a : a + 1] for a in range(4)], axis=1)
        cross_sum = jnp.concatenate([total[4 + a : 5 + a] for a in range(4)], axis=1)
        inverse = lax.rsqrt(square_sum / D + EPS)
        cross_mean = cross_sum / D
        weighted = cotb[s].astype(F32) * gain[...]
        grad_hidden = (inverse * weighted - HID[...] * (inverse * inverse * inverse * cross_mean)).astype(BF)
        for j in range(CH):
            gradient = jnp.dot(grad_hidden, context_block(s, j), preferred_element_type=F32) * SCALE
            FM[s, j] = (DECAY * MB[s, j].astype(F32) + gradient).astype(BF)
            fm_copy(s, j).start()
            if j % 2:
                pump()
        for j in range(CH):
            if j == CH - 1 and s + 1 < STEPS:
                gathered(s + 1)
                for i in range(CH - 1):
                    project(s + 1, i)
            else:
                pump(2)
            w_copy(s, j).wait_recv()
            fm_copy(s, j).wait_recv()
            fresh, theirs = FM[s, j].astype(F32), RM[s, j].astype(F32)
            fresh_w = (WB[s, j].astype(F32) - LEARN * fresh).astype(BF).astype(F32)
            their_w = (RW[s, j].astype(F32) - LEARN * theirs).astype(BF).astype(F32)
            WB[s + 1, j] = ((fresh_w + their_w) * 0.5).astype(BF)
            MB[s + 1, j] = ((fresh + theirs) * 0.5).astype(BF)
            if s + 1 < STEPS:
                w_copy(s + 1, j).start()
                if j == CH - 1:
                    project(s + 1, j)
            else:
                cols = pl.ds(WIDE * j, WIDE)
                pltpu.make_async_copy(WB.at[STEPS, j], w_out.at[0, :, cols], outs.at[0, j]).start()
                pltpu.make_async_copy(MB.at[STEPS, j], m_out.at[0, :, cols], outs.at[1, j]).start()

    for j in range(CH):
        cols = pl.ds(WIDE * j, WIDE)
        pltpu.make_async_copy(WB.at[STEPS, j], w_out.at[0, :, cols], outs.at[0, j]).wait()
        pltpu.make_async_copy(MB.at[STEPS, j], m_out.at[0, :, cols], outs.at[1, j]).wait()
    for s in range(STEPS):
        sent = G.at[s, pl.ds(0, 2 * ROUNDS)]
        remote(sent, sent, ring_s.at[s], ring_r.at[s, 0, 0, 0], up).wait_send()
        sent = G.at[s, pl.ds(0, 15)]
        remote(sent, sent, sib_s.at[s], sib_r.at[s], sibling).wait_send()
        remote(FM.at[s], RM.at[s], fm_s.at[s], fm_r.at[s, 0], peers[s]).wait_send()
        remote(RW.at[s], RW.at[s], w_s.at[s], w_r.at[s, 0], peers[s]).wait_send()
        others = SB.at[s, pl.ds(0, TP - 1)]
        remote(others, others, sum_s.at[s], sum_r.at[s], sibling).wait_send()


def run(number, bits, operands):
    anywhere = pl.BlockSpec(memory_space=pl.ANY)
    dma = pltpu.SemaphoreType.DMA
    shard = jax.ShapeDtypeStruct((1, ROWS, HF), BF)
    chunks = (CH, ROWS, WIDE)
    return pl.pallas_call(
        functools.partial(kernel, bits),
        out_shape=(shard, shard),
        in_specs=[anywhere] * 3 + [pl.BlockSpec(memory_space=pltpu.VMEM)] + [anywhere] * 2,
        out_specs=(anywhere, anywhere),
        scratch_shapes=[
            pltpu.VMEM((STEPS, 2 * TP, TOK, HF), BF),
            pltpu.VMEM((STEPS + 1, *chunks), BF),
            pltpu.VMEM((STEPS + 1, *chunks), BF),
            pltpu.VMEM((STEPS, *chunks), BF),
            pltpu.VMEM((STEPS, *chunks), BF),
            pltpu.VMEM((STEPS, *chunks), BF),
            pltpu.VMEM((STEPS, ROWS, SEQ), BF),
            pltpu.VMEM((STEPS, ROWS, SEQ), BF),
            pltpu.VMEM((ROWS, SEQ), F32),
            pltpu.VMEM((STEPS, TP, 8, 128), F32),
            dma((STEPS, 2, ROUNDS, 2)),
            dma((STEPS,)),
            dma((STEPS,)),
            dma((STEPS,)),
            dma((2 * CH + 2 + STEPS,)),
            dma((STEPS, CH)),
            dma((STEPS,)),
            dma((STEPS, CH)),
            dma((STEPS,)),
            dma((STEPS,)),
            dma((STEPS,)),
            dma((2, CH)),
        ],
        compiler_params=pltpu.CompilerParams(
            collective_id=number, has_side_effects=True, vmem_limit_bytes=56 << 20
        ),
        name=f"window_{number}",
    )(*operands)


def on_device(context, residual, cotangent, norm_gain, weight, momentum, round_start):
    count = lax.axis_size("rep").bit_length() - 1
    gain = norm_gain.astype(F32)[:, None]
    branches = [
        functools.partial(run, first, tuple((first + s) % count for s in range(STEPS)))
        for first in range(count)
    ]
    return lax.switch(
        round_start[0] % count, [lambda *o, f=f: f(o) for f in branches],
        context, residual, cotangent, gain, weight, momentum,
    )


def solution(mesh):
    return jax.shard_map(
        on_device,
        mesh=mesh,
        in_specs=(
            P("rep", None, "tp", None),
            P("rep", None, "tp", None),
            P("rep", None, "tp", None),
            P("tp"),
            P("rep", "tp", None),
            P("rep", "tp", None),
            P(),
        ),
        out_specs=(P("rep", "tp", None), P("rep", "tp", None)),
        check_vma=False,
    )
```

```python
import functools

import jax
import jax.numpy as jnp
from jax import lax
from jax.experimental import pallas as pl
from jax.experimental.pallas import tpu as pltpu
from jax.sharding import PartitionSpec as P

D = 2560
HF = 2560
SEQ = 512
STEPS = 3
TP = 16
ROWS = D // TP
TOK = SEQ // TP
WIDE = 640
CH = HF // WIDE
ROUNDS = 7
HALF = TOK // 2
LEARN = 0.5
DECAY = 0.9
EPS = 1e-05
SCALE = HF**-0.5
MESH = pl.DeviceIdType.MESH
BF = jnp.bfloat16
F32 = jnp.float32
BLOCK = 32


def remote(src, dst, send, recv, device):
    return pltpu.make_async_remote_copy(
        src_ref=src, dst_ref=dst, send_sem=send, recv_sem=recv, device_id=device, device_id_type=MESH
    )


def by_rows(body):
    @pl.loop(0, ROWS // BLOCK)
    def _(i):
        body(pl.ds(pl.multiple_of(i * BLOCK, BLOCK), BLOCK))


def kernel(bits, ctx, res, cot, gain, weight, moment, w_out, m_out, *scratch):
    (
        G, WB, MB, FM, RW, RM, resb, cotb, HID, SB,
        ring_r, ring_s, sib_r, sib_s, loc, fm_r, fm_s, w_r, w_s, sum_r, sum_s, outs,
    ) = scratch[:22]
    lazy = 0 in bits
    zs = bits.index(0) if lazy else 2 * STEPS
    ts = min(zs, 1) if lazy else 2 * STEPS
    if lazy:
        (
            BB, HB, GH, GHQ, V, U, RU, YB, YR, TPB, RT, TS, RTS, TM,
            gh_r, gh_s, y_r, y_s, u_r, u_s, rt_r, rt_s, ts_r, ts_s, tm_r, tm_s,
        ) = scratch[22:]
    rep = lax.axis_index("rep")
    tp = lax.axis_index("tp")
    core = tp % 2
    z_hi = rep % 2
    z = z_hi * 8 + tp // 2
    base = rep - z_hi

    def at_z(place):
        return (base + place // 8, (place % 8) * 2 + core)

    up_z, down_z = (z + 1) % 16, (z + 15) % 16
    up, down = at_z(up_z), at_z(down_z)
    sibling = (rep, tp + 1 - 2 * core)

    def bit_of(bit):
        return (rep // (1 << bit)) % 2

    def flipped(*which):
        other = rep
        for bit in which:
            d = 1 << bit
            other = other + d - 2 * d * bit_of(bit)
        return (other, tp)

    peers = [flipped(b) for b in bits]
    pair = flipped(0)
    greet = [(rep, (tp + j) % TP) for j in range(1, TP)] + [up, down] + peers
    if lazy:
        first, second = [b for b in bits if b != 0]
        quarter = bit_of(first) + 2 * bit_of(second)
        flips = [(first,), (second,), (first, second)]
        late = [b for b in bits[ts:] if b != 0]
        apart = [m for m in range(3) if all(b in late for b in flips[m])]
        quad = [flipped(*f) for f in flips]
        quad_quarter = [
            (1 - bit_of(first) if first in f else bit_of(first))
            + 2 * (1 - bit_of(second) if second in f else bit_of(second))
            for f in flips
        ]
        greet.append(quad[2])

    def wide(j):
        return pl.ds(pl.multiple_of(j * WIDE, WIDE), WIDE)

    loads = []
    for j in range(CH):
        loads.append(pltpu.make_async_copy(weight.at[0, :, wide(j)], WB.at[0, j], loc.at[j]))
        loads.append(pltpu.make_async_copy(moment.at[0, :, wide(j)], MB.at[0, j], loc.at[CH + j]))
    loads.append(pltpu.make_async_copy(res.at[0], resb, loc.at[2 * CH]))
    loads.append(pltpu.make_async_copy(cot.at[0], cotb, loc.at[2 * CH + 1]))
    for s in range(STEPS):
        loads.append(pltpu.make_async_copy(ctx.at[0, s], G.at[s, tp], loc.at[2 * CH + 2 + s]))
    for c in loads:
        c.start()

    barrier = pltpu.get_barrier_semaphore()
    for d in greet:
        pl.semaphore_signal(barrier, inc=1, device_id=d, device_id_type=MESH)
    pl.semaphore_wait(barrier, len(greet))

    far = [lazy and s >= ts for s in range(STEPS)]

    def slot(origin, receiver_z):
        return ((origin // 8 + receiver_z // 8) % 2) * 16 + (origin % 8) * 2 + core

    def ring(s, way, k, h):
        origin = (z + 16 - (k - 1)) % 16 if way == 0 else (z + (k - 1)) % 16
        target, target_z = (up, up_z) if way == 0 else (down, down_z)
        rows = pl.ds(HALF * h, HALF)
        src = ctx.at[0, s, rows] if k == 1 else G.at[s, slot(origin, z), rows]
        return remote(
            src, G.at[s, slot(origin, target_z), rows], ring_s.at[s], ring_r.at[s, way, k - 1, h], target
        )

    def to_sibling(s, way, k):
        origin = (z + 16 - k) % 16 if way == 0 else (z + k) % 16
        place = slot(origin, z)
        return remote(G.at[s, place], G.at[s, place], sib_s.at[s], sib_r.at[s], sibling)

    def pumps():
        for s in range(STEPS):
            for k in range(1, ROUNDS + 1):
                for h in (0, 1):
                    for way in (0, 1):
                        if k > 1:
                            ring(s, way, k - 1, h).wait_recv()
                        ring(s, way, k, h).start()
                    if k > 1 and h == 1:
                        for way in (0, 1):
                            to_sibling(s, way, k - 1).start()
                    if k == 1 and h == 1:
                        remote(ctx.at[0, s], G.at[s, tp], sib_s.at[s], sib_r.at[s], sibling).start()
                    yield s
            for h in (0, 1):
                for way in (0, 1):
                    ring(s, way, ROUNDS, h).wait_recv()
                    if far[s] and way == h:
                        ring(s, way, ROUNDS + 1, h).start()
            for way in (0, 1):
                to_sibling(s, way, ROUNDS).start()
            yield s
            if far[s]:
                for way in (0, 1):
                    ring(s, way, ROUNDS + 1, way).wait_recv()
                to_sibling(s, 0, ROUNDS + 1).start()
                yield s

    ends = [sum(2 * ROUNDS + 1 + far[i] for i in range(s + 1)) for s in range(STEPS)]
    state = {"gen": pumps(), "count": 0}

    def pump(n=1):
        for _ in range(n):
            if state["count"] < ends[-1]:
                next(state["gen"])
                state["count"] += 1

    arrived = set()

    def gathered(s):
        if s in arrived:
            return
        arrived.add(s)
        while state["count"] < ends[s]:
            pump()
        whole = G.at[s, pl.ds(0, 15 + far[s])]
        remote(whole, whole, sib_s.at[s], sib_r.at[s], sibling).wait_recv()

    def context_block(s, j, group=0):
        return G[s, 16 * group : 16 * group + 16, :, wide(j)].reshape(SEQ, WIDE)

    def fm_copy(s, j):
        return remote(FM.at[s, j], RM.at[s, j], fm_s.at[s], fm_r.at[s, j], peers[s])

    def state_w(s):
        return BB if s > zs else WB

    def state_m(s):
        return HB if s > zs else MB

    def w_copy(s, j):
        src = weight.at[0, :, wide(j)] if s == 0 else state_w(s).at[s, j]
        return remote(src, RW.at[s, j], w_s.at[s], w_r.at[s, j], peers[s])

    nt = (((1,), (1,)), ((), ()))

    def project(s, source, group=0):
        HID[...] = jnp.zeros_like(HID)

        @pl.loop(0, CH)
        def _(j):
            block = context_block(s, j, group)
            for ref, factor in source:
                part = lax.dot_general(ref[j], block, nt, preferred_element_type=F32)
                HID[...] += part if factor == 1.0 else part * factor

    if lazy:
        span = STEPS - ts
        after = STEPS - 1 - zs
        c_p = LEARN * sum(DECAY**n for n in range(1, span + 1))
        c_q = DECAY**span

        def mean_start():
            @pl.loop(0, CH)
            def _(j):
                def rows(i):
                    w, m = WB[ts, j, i].astype(F32), MB[ts, j, i].astype(F32)
                    TPB[j, 0, i] = (w - c_p * m).astype(BF)
                    TPB[j, 1, i] = (c_q * m).astype(BF)
                    if after > 0:
                        V[0, j, i] = (w - (LEARN * DECAY) * m).astype(BF)
                    if after > 1:
                        U[j, i] = (w - (LEARN * (DECAY + DECAY**2)) * m).astype(BF)

                by_rows(rows)

            if after > 1:
                remote(U, RU, u_s, u_r, peers[1]).start()
            for m in apart:
                remote(TPB.at[quad_quarter[m]], RT.at[m], rt_s.at[m], rt_r.at[m], quad[m]).start()

        def mean_cross():
            for m in apart:
                remote(TPB.at[quad_quarter[m]], RT.at[m], rt_s.at[m], rt_r.at[m], quad[m]).wait_recv()
            for i in range(2):

                def rows(r, i=i):
                    total = TPB[quarter, i, r].astype(F32)
                    for m in apart:
                        total += RT[m, i, r].astype(F32)
                    TS[i, r] = (total * (1.0 / (1 + len(apart)))).astype(BF)

                by_rows(rows)
                remote(TS.at[i], RTS.at[i], ts_s.at[i], ts_r.at[i], pair).start()

        def tm_copy(m, i, place):
            return remote(TM.at[place, i], TM.at[place, i], tm_s.at[m, i], tm_r.at[m, i], quad[m])

        def mean_spread():
            for i in range(2):
                remote(TS.at[i], RTS.at[i], ts_s.at[i], ts_r.at[i], pair).wait_recv()

                def rows(r, i=i):
                    TM[quarter, i, r] = ((TS[i, r].astype(F32) + RTS[i, r].astype(F32)) * 0.5).astype(BF)

                by_rows(rows)
                for m in range(3):
                    tm_copy(m, i, quarter).start()

        def mean_done():
            for m in range(3):
                for i in range(2):
                    tm_copy(m, i, quarter).wait_recv()

        def y_copy(n):
            return remote(YB.at[n], YR.at[n], y_s.at[n], y_r.at[n], pair)

        def cross_project(s):
            n = s - zs - 1
            gathered(s)
            if n == 1:
                remote(U, RU, u_s, u_r, peers[1]).wait_recv()

                @pl.loop(0, CH)
                def _(j):
                    def rows(i):
                        V[1, j, i] = ((U[j, i].astype(F32) + RU[j, i].astype(F32)) * 0.5).astype(BF)

                    by_rows(rows)

            project(s, [(V.at[n], 1.0)], 1)
            YB[n] = HID[...].astype(BF)
            y_copy(n).start()

    if lazy:
        swap = remote(GH.at[0], GHQ.at[0], gh_s.at[0], gh_r.at[0], pair)
    if zs == 2:
        early = remote(GH.at[1], GHQ.at[1], gh_s.at[1], gh_r.at[1], pair)

    pump(2)
    if zs > 0:
        for j in range(CH):
            w_copy(0, j).start()
    for c in loads:
        c.wait()
    if zs == 0:
        mean_start()
    gathered(0)
    pump(2)

    for s in range(STEPS):
        gathered(s)
        if s > zs:
            n = s - zs - 1
            project(s, [(V.at[n], 0.5), (state_w(s).at[s], 1.0)])
            if s == 1:
                pump(8)
            y_copy(n).wait_recv()
            hidden = (HID[...] + 0.5 * YR[n].astype(F32)) * SCALE + resb[s].astype(F32)
        else:
            project(s, [(state_w(s).at[s], 1.0)])
            hidden = HID[...] * SCALE + resb[s].astype(F32)
        HID[...] = hidden
        weighted = cotb[s].astype(F32) * gain[...]
        squares = jnp.sum(hidden * hidden, axis=0, keepdims=True)
        crosses = jnp.sum(weighted * hidden, axis=0, keepdims=True)
        SB[s, TP - 1] = jnp.concatenate(
            [v[:, 128 * a : 128 * (a + 1)] for v in (squares, crosses) for a in range(4)], axis=0
        )

        @pl.loop(1, TP)
        def _(j):
            remote(
                SB.at[s, TP - 1], SB.at[s, j - 1], sum_s.at[s], sum_r.at[s], (rep, (tp + j) % TP)
            ).start()

        pump(4)
        others = SB.at[s, pl.ds(0, TP - 1)]
        remote(others, others, sum_s.at[s], sum_r.at[s], sibling).wait_recv()
        total = jnp.sum(SB[s], axis=0)
        square_sum = jnp.concatenate([total[a : a + 1] for a in range(4)], axis=1)
        cross_sum = jnp.concatenate([total[4 + a : 5 + a] for a in range(4)], axis=1)
        inverse = lax.rsqrt(square_sum / D + EPS)
        cross_mean = cross_sum / D
        weighted = cotb[s].astype(F32) * gain[...]
        grad_hidden = (inverse * weighted - HID[...] * (inverse * inverse * inverse * cross_mean)).astype(BF)

        if s == zs:
            GH[0] = grad_hidden
            swap.start()
            if s + 1 < STEPS:
                cross_project(s + 1)
                if zs == 1:
                    mean_cross()
            else:
                mean_spread()
            swap.wait_recv()
            if zs == 2:
                remote(U, RU, u_s, u_r, peers[1]).wait_recv()

            @pl.loop(0, CH)
            def _(j):
                mine = jnp.dot(GH[0], context_block(s, j), preferred_element_type=F32)
                theirs = jnp.dot(GHQ[0], context_block(s, j, 1), preferred_element_type=F32)
                both = (mine + theirs) * (0.5 * SCALE)
                if zs == 2:
                    older = (U[j].astype(F32) + RU[j].astype(F32)) * 0.5
                    HB[s + 1, j] = (both + DECAY * older).astype(BF)
                    BB[s + 1, j] = (both * -LEARN - (LEARN * (1 + DECAY)) * older).astype(BF)
                else:
                    HB[s + 1, j] = both.astype(BF)
                    BB[s + 1, j] = (both * -LEARN).astype(BF)

            if s + 1 < STEPS:
                for j in range(CH):
                    w_copy(s + 1, j).start()
        else:
            GH2 = FM.at[s]

            @pl.loop(0, CH)
            def _(j):
                gradient = jnp.dot(grad_hidden, context_block(s, j), preferred_element_type=F32) * SCALE
                GH2[j] = (DECAY * state_m(s)[s, j].astype(F32) + gradient).astype(BF)
                fm_copy(s, j).start()

            if zs == 0 and s == 1:
                cross_project(2)
                mean_cross()
            if zs == 2 and s == 1:
                GH[1] = grad_hidden
                early.start()
            for j in range(CH):
                pump(3)
                if zs == 2 and s == 1 and j == CH - 2:
                    gathered(2)
                    mean_cross()
                w_copy(s, j).wait_recv()
                fm_copy(s, j).wait_recv()

                def rows(i, j=j):
                    fresh, theirs = FM[s, j, i].astype(F32), RM[s, j, i].astype(F32)
                    fresh_w = (state_w(s)[s, j, i].astype(F32) - LEARN * fresh).astype(BF).astype(F32)
                    their_w = (RW[s, j, i].astype(F32) - LEARN * theirs).astype(BF).astype(F32)
                    new_w = (fresh_w + their_w) * 0.5
                    new_m = (fresh + theirs) * 0.5
                    state_w(s)[s + 1, j, i] = new_w.astype(BF)
                    state_m(s)[s + 1, j, i] = new_m.astype(BF)

                by_rows(rows)
                if s + 1 < STEPS and s + 1 != zs:
                    w_copy(s + 1, j).start()
                elif not lazy:
                    pltpu.make_async_copy(WB.at[STEPS, j], w_out.at[0, :, wide(j)], outs.at[0, j]).start()
                    pltpu.make_async_copy(MB.at[STEPS, j], m_out.at[0, :, wide(j)], outs.at[1, j]).start()
            if s + 1 == ts:
                mean_start()
            if s > zs and s == STEPS - 1:
                mean_spread()
            if zs == 2 and s == 1:
                early.wait_recv()

                @pl.loop(0, CH)
                def _(j):
                    mine = jnp.dot(GH[1], context_block(s, j), preferred_element_type=F32)
                    theirs = jnp.dot(GHQ[1], context_block(s, j, 1), preferred_element_type=F32)
                    U[j] = ((mine + theirs) * (0.5 * SCALE)).astype(BF)

                remote(U, RU, u_s, u_r, peers[1]).start()

    if lazy:
        mean_done()
        for j in range(CH):

            def rows(i, j=j):
                WB[0, j, i] = (TM[j, 0, i].astype(F32) + BB[STEPS, j, i].astype(F32)).astype(BF)
                MB[0, j, i] = (TM[j, 1, i].astype(F32) + HB[STEPS, j, i].astype(F32)).astype(BF)

            by_rows(rows)
            pltpu.make_async_copy(WB.at[0, j], w_out.at[0, :, wide(j)], outs.at[0, j]).start()
            pltpu.make_async_copy(MB.at[0, j], m_out.at[0, :, wide(j)], outs.at[1, j]).start()
    last = 0 if lazy else STEPS
    for j in range(CH):
        pltpu.make_async_copy(WB.at[last, j], w_out.at[0, :, wide(j)], outs.at[0, j]).wait()
        pltpu.make_async_copy(MB.at[last, j], m_out.at[0, :, wide(j)], outs.at[1, j]).wait()
    for s in range(STEPS):
        sent = G.at[s, pl.ds(0, 2 * ROUNDS + far[s])]
        remote(sent, sent, ring_s.at[s], ring_r.at[s, 0, 0, 0], up).wait_send()
        sent = G.at[s, pl.ds(0, 15 + far[s])]
        remote(sent, sent, sib_s.at[s], sib_r.at[s], sibling).wait_send()
        if s != zs:
            remote(FM.at[s], RM.at[s], fm_s.at[s], fm_r.at[s, 0], peers[s]).wait_send()
            remote(RW.at[s], RW.at[s], w_s.at[s], w_r.at[s, 0], peers[s]).wait_send()
        others = SB.at[s, pl.ds(0, TP - 1)]
        remote(others, others, sum_s.at[s], sum_r.at[s], sibling).wait_send()
    if lazy:
        swap.wait_send()
        if zs == 2:
            early.wait_send()
        for n in range(after):
            y_copy(n).wait_send()
        if after != 1:
            remote(U, RU, u_s, u_r, peers[1]).wait_send()
        for m in apart:
            remote(TPB.at[quad_quarter[m]], RT.at[m], rt_s.at[m], rt_r.at[m], quad[m]).wait_send()
        for i in range(2):
            remote(TS.at[i], RTS.at[i], ts_s.at[i], ts_r.at[i], pair).wait_send()
            for m in range(3):
                tm_copy(m, i, quarter).wait_send()


def run(number, bits, operands):
    anywhere = pl.BlockSpec(memory_space=pl.ANY)
    dma = pltpu.SemaphoreType.DMA
    shard = jax.ShapeDtypeStruct((1, ROWS, HF), BF)
    chunks = (CH, ROWS, WIDE)
    lazy = 0 in bits
    many = STEPS if lazy else STEPS + 1
    scratch = [
        pltpu.VMEM((STEPS, 2 * TP, TOK, HF), BF),
        pltpu.VMEM((many, *chunks), BF),
        pltpu.VMEM((many, *chunks), BF),
        pltpu.VMEM((STEPS, *chunks), BF),
        pltpu.VMEM((STEPS, *chunks), BF),
        pltpu.VMEM((STEPS, *chunks), BF),
        pltpu.VMEM((STEPS, ROWS, SEQ), BF),
        pltpu.VMEM((STEPS, ROWS, SEQ), BF),
        pltpu.VMEM((ROWS, SEQ), F32),
        pltpu.VMEM((STEPS, TP, 8, 128), F32),
        dma((STEPS, 2, ROUNDS + 1, 2)),
        dma((STEPS,)),
        dma((STEPS,)),
        dma((STEPS,)),
        dma((2 * CH + 2 + STEPS,)),
        dma((STEPS, CH)),
        dma((STEPS,)),
        dma((STEPS, CH)),
        dma((STEPS,)),
        dma((STEPS,)),
        dma((STEPS,)),
        dma((2, CH)),
    ]
    if lazy:
        tile = (ROWS, SEQ)
        part = (2, ROWS, WIDE)
        scratch += [
            pltpu.VMEM((STEPS + 1, *chunks), BF),
            pltpu.VMEM((STEPS + 1, *chunks), BF),
            pltpu.VMEM((2, *tile), BF),
            pltpu.VMEM((2, *tile), BF),
            pltpu.VMEM((2, *chunks), BF),
            pltpu.VMEM(chunks, BF),
            pltpu.VMEM(chunks, BF),
            pltpu.VMEM((2, *tile), BF),
            pltpu.VMEM((2, *tile), BF),
            pltpu.VMEM((CH, *part), BF),
            pltpu.VMEM((3, *part), BF),
            pltpu.VMEM(part, BF),
            pltpu.VMEM(part, BF),
            pltpu.VMEM((CH, *part), BF),
            dma((2,)), dma((2,)), dma((2,)), dma((2,)), dma, dma,
            dma((3,)), dma((3,)), dma((2,)), dma((2,)), dma((3, 2)), dma((3, 2)),
        ]
    return pl.pallas_call(
        functools.partial(kernel, bits),
        out_shape=(shard, shard),
        in_specs=[anywhere] * 3 + [pl.BlockSpec(memory_space=pltpu.VMEM)] + [anywhere] * 2,
        out_specs=(anywhere, anywhere),
        scratch_shapes=scratch,
        compiler_params=pltpu.CompilerParams(
            collective_id=number, has_side_effects=True, vmem_limit_bytes=58 << 20
        ),
        name=f"window_{number}",
    )(*operands)


def on_device(context, residual, cotangent, norm_gain, weight, momentum, round_start):
    count = lax.axis_size("rep").bit_length() - 1
    gain = norm_gain.astype(F32)[:, None]
    branches = [
        functools.partial(run, first, tuple((first + s) % count for s in range(STEPS)))
        for first in range(count)
    ]
    return lax.switch(
        round_start[0] % count, [lambda *o, f=f: f(o) for f in branches],
        context, residual, cotangent, gain, weight, momentum,
    )


def solution(mesh):
    return jax.shard_map(
        on_device,
        mesh=mesh,
        in_specs=(
            P("rep", None, "tp", None),
            P("rep", None, "tp", None),
            P("rep", None, "tp", None),
            P("tp"),
            P("rep", "tp", None),
            P("rep", "tp", None),
            P(),
        ),
        out_specs=(P("rep", "tp", None), P("rep", "tp", None)),
        check_vma=False,
    )
```

```python
import functools

import jax
import jax.numpy as jnp
from jax import lax
from jax.experimental import pallas as pl
from jax.experimental.pallas import tpu as pltpu
from jax.sharding import PartitionSpec as P

D = 2560
HF = 2560
SEQ = 512
STEPS = 3
TP = 16
ROWS = D // TP
TOK = SEQ // TP
WIDE = 640
CH = HF // WIDE
ROUNDS = 7
HALF = TOK // 2
LEARN = 0.5
DECAY = 0.9
EPS = 1e-05
SCALE = HF**-0.5
MESH = pl.DeviceIdType.MESH
BF = jnp.bfloat16
F32 = jnp.float32
BLOCK = 32


def remote(src, dst, send, recv, device):
    return pltpu.make_async_remote_copy(
        src_ref=src, dst_ref=dst, send_sem=send, recv_sem=recv, device_id=device, device_id_type=MESH
    )


def by_rows(body):
    @pl.loop(0, ROWS // BLOCK)
    def _(i):
        body(pl.ds(pl.multiple_of(i * BLOCK, BLOCK), BLOCK))


def kernel(bits, ctx, res, cot, gain, weight, moment, w_out, m_out, *scratch):
    (
        G, WB, MB, FM, RW, RM, resb, cotb, HID, SB,
        ring_r, ring_s, sib_r, sib_s, loc, fm_r, fm_s, w_r, w_s, sum_r, sum_s, outs,
    ) = scratch[:22]
    lazy = 0 in bits
    zs = bits.index(0) if lazy else 2 * STEPS
    ts = min(zs, 1) if lazy else 2 * STEPS
    if lazy:
        (
            BB, HB, GH, GHQ, V, U, RU, YB, YR, TPB, RT, TS, RTS, TM,
            gh_r, gh_s, y_r, y_s, u_r, u_s, rt_r, rt_s, ts_r, ts_s, tm_r, tm_s,
        ) = scratch[22:]
    rep = lax.axis_index("rep")
    tp = lax.axis_index("tp")
    core = tp % 2
    z_hi = rep % 2
    z = z_hi * 8 + tp // 2
    base = rep - z_hi

    def at_z(place):
        return (base + place // 8, (place % 8) * 2 + core)

    up_z, down_z = (z + 1) % 16, (z + 15) % 16
    up, down = at_z(up_z), at_z(down_z)
    sibling = (rep, tp + 1 - 2 * core)

    def bit_of(bit):
        return (rep // (1 << bit)) % 2

    def flipped(*which):
        other = rep
        for bit in which:
            d = 1 << bit
            other = other + d - 2 * d * bit_of(bit)
        return (other, tp)

    peers = [flipped(b) for b in bits]
    pair = flipped(0)
    greet = [(rep, (tp + j) % TP) for j in range(1, TP)] + [up, down] + peers
    if lazy:
        first, second = [b for b in bits if b != 0]
        quarter = bit_of(first) + 2 * bit_of(second)
        flips = [(first,), (second,), (first, second)]
        late = [b for b in bits[ts:] if b != 0]
        apart = [m for m in range(3) if all(b in late for b in flips[m])]
        quad = [flipped(*f) for f in flips]
        quad_quarter = [
            (1 - bit_of(first) if first in f else bit_of(first))
            + 2 * (1 - bit_of(second) if second in f else bit_of(second))
            for f in flips
        ]
        greet.append(quad[2])

    def wide(j):
        return pl.ds(pl.multiple_of(j * WIDE, WIDE), WIDE)

    loads = []
    for j in range(CH):
        loads.append(pltpu.make_async_copy(weight.at[0, :, wide(j)], WB.at[0, j], loc.at[j]))
        loads.append(pltpu.make_async_copy(moment.at[0, :, wide(j)], MB.at[0, j], loc.at[CH + j]))
    loads.append(pltpu.make_async_copy(res.at[0], resb, loc.at[2 * CH]))
    loads.append(pltpu.make_async_copy(cot.at[0], cotb, loc.at[2 * CH + 1]))
    for s in range(STEPS):
        loads.append(pltpu.make_async_copy(ctx.at[0, s], G.at[s, tp], loc.at[2 * CH + 2 + s]))
    for c in loads:
        c.start()

    barrier = pltpu.get_barrier_semaphore()
    for d in greet:
        pl.semaphore_signal(barrier, inc=1, device_id=d, device_id_type=MESH)
    pl.semaphore_wait(barrier, len(greet))

    far = [lazy and s >= ts for s in range(STEPS)]

    def slot(origin, receiver_z):
        return ((origin // 8 + receiver_z // 8) % 2) * 16 + (origin % 8) * 2 + core

    def ring(s, way, k, h):
        origin = (z + 16 - (k - 1)) % 16 if way == 0 else (z + (k - 1)) % 16
        target, target_z = (up, up_z) if way == 0 else (down, down_z)
        rows = pl.ds(HALF * h, HALF)
        src = ctx.at[0, s, rows] if k == 1 else G.at[s, slot(origin, z), rows]
        return remote(
            src, G.at[s, slot(origin, target_z), rows], ring_s.at[s], ring_r.at[s, way, k - 1, h], target
        )

    def to_sibling(s, way, k):
        origin = (z + 16 - k) % 16 if way == 0 else (z + k) % 16
        place = slot(origin, z)
        return remote(G.at[s, place], G.at[s, place], sib_s.at[s], sib_r.at[s], sibling)

    def pumps():
        for s in range(STEPS):
            for k in range(1, ROUNDS + 1):
                for h in (0, 1):
                    for way in (0, 1):
                        if k > 1:
                            ring(s, way, k - 1, h).wait_recv()
                        ring(s, way, k, h).start()
                    if k > 1 and h == 1:
                        for way in (0, 1):
                            to_sibling(s, way, k - 1).start()
                    if k == 1 and h == 1:
                        remote(ctx.at[0, s], G.at[s, tp], sib_s.at[s], sib_r.at[s], sibling).start()
                    yield s
            for h in (0, 1):
                for way in (0, 1):
                    ring(s, way, ROUNDS, h).wait_recv()
                    if far[s] and way == h:
                        ring(s, way, ROUNDS + 1, h).start()
            for way in (0, 1):
                to_sibling(s, way, ROUNDS).start()
            yield s
            if far[s]:
                for way in (0, 1):
                    ring(s, way, ROUNDS + 1, way).wait_recv()
                to_sibling(s, 0, ROUNDS + 1).start()
                yield s

    ends = [sum(2 * ROUNDS + 1 + far[i] for i in range(s + 1)) for s in range(STEPS)]
    state = {"gen": pumps(), "count": 0}

    def pump(n=1):
        for _ in range(n):
            if state["count"] < ends[-1]:
                next(state["gen"])
                state["count"] += 1

    arrived = set()

    def gathered(s):
        if s in arrived:
            return
        arrived.add(s)
        while state["count"] < ends[s]:
            pump()
        whole = G.at[s, pl.ds(0, 15 + far[s])]
        remote(whole, whole, sib_s.at[s], sib_r.at[s], sibling).wait_recv()

    def context_block(s, j, group=0):
        return G[s, 16 * group : 16 * group + 16, :, wide(j)].reshape(SEQ, WIDE)

    def fm_copy(s, j):
        return remote(FM.at[s, j], RM.at[s, j], fm_s.at[s], fm_r.at[s, j], peers[s])

    def state_w(s):
        return BB if s > zs else WB

    def state_m(s):
        return HB if s > zs else MB

    def w_copy(s, j):
        src = weight.at[0, :, wide(j)] if s == 0 else state_w(s).at[s, j]
        return remote(src, RW.at[s, j], w_s.at[s], w_r.at[s, j], peers[s])

    nt = (((1,), (1,)), ((), ()))

    def project(s, source, group=0):
        HID[...] = jnp.zeros_like(HID)

        @pl.loop(0, CH)
        def _(j):
            block = context_block(s, j, group)
            for ref, factor in source:
                part = lax.dot_general(ref[j], block, nt, preferred_element_type=F32)
                HID[...] += part if factor == 1.0 else part * factor

    if lazy:
        span = STEPS - ts
        after = STEPS - 1 - zs
        c_p = LEARN * sum(DECAY**n for n in range(1, span + 1))
        c_q = DECAY**span

        def mean_start():
            @pl.loop(0, CH)
            def _(j):
                def rows(i):
                    w, m = WB[ts, j, i].astype(F32), MB[ts, j, i].astype(F32)
                    TPB[j, 0, i] = (w - c_p * m).astype(BF)
                    TPB[j, 1, i] = (c_q * m).astype(BF)
                    if after > 0:
                        V[0, j, i] = (w - (LEARN * DECAY) * m).astype(BF)
                    if after > 1:
                        U[j, i] = (w - (LEARN * (DECAY + DECAY**2)) * m).astype(BF)

                by_rows(rows)

            if after > 1:
                remote(U, RU, u_s, u_r, peers[1]).start()
            for m in apart:
                remote(TPB.at[quad_quarter[m]], RT.at[m], rt_s.at[m], rt_r.at[m], quad[m]).start()

        def mean_cross():
            for m in apart:
                remote(TPB.at[quad_quarter[m]], RT.at[m], rt_s.at[m], rt_r.at[m], quad[m]).wait_recv()
            for i in range(2):

                def rows(r, i=i):
                    total = TPB[quarter, i, r].astype(F32)
                    for m in apart:
                        total += RT[m, i, r].astype(F32)
                    TS[i, r] = (total * (1.0 / (1 + len(apart)))).astype(BF)

                by_rows(rows)
                remote(TS.at[i], RTS.at[i], ts_s.at[i], ts_r.at[i], pair).start()

        def tm_copy(m, i, place):
            return remote(TM.at[place, i], TM.at[place, i], tm_s.at[m, i], tm_r.at[m, i], quad[m])

        def mean_spread():
            for i in range(2):
                remote(TS.at[i], RTS.at[i], ts_s.at[i], ts_r.at[i], pair).wait_recv()

                def rows(r, i=i):
                    TM[quarter, i, r] = ((TS[i, r].astype(F32) + RTS[i, r].astype(F32)) * 0.5).astype(BF)

                by_rows(rows)
                for m in range(3):
                    tm_copy(m, i, quarter).start()

        def mean_done():
            for m in range(3):
                for i in range(2):
                    tm_copy(m, i, quarter).wait_recv()

        def y_copy(n):
            return remote(YB.at[n], YR.at[n], y_s.at[n], y_r.at[n], pair)

        def cross_project(s):
            n = s - zs - 1
            gathered(s)
            if n == 1:
                remote(U, RU, u_s, u_r, peers[1]).wait_recv()

                @pl.loop(0, CH)
                def _(j):
                    def rows(i):
                        V[1, j, i] = ((U[j, i].astype(F32) + RU[j, i].astype(F32)) * 0.5).astype(BF)

                    by_rows(rows)

            project(s, [(V.at[n], 1.0)], 1)
            YB[n] = HID[...].astype(BF)
            y_copy(n).start()

    if lazy:
        swap = remote(GH.at[0], GHQ.at[0], gh_s.at[0], gh_r.at[0], pair)
    if zs == 2:
        early = remote(GH.at[1], GHQ.at[1], gh_s.at[1], gh_r.at[1], pair)

    pump(2)
    if zs > 0:
        for j in range(CH):
            w_copy(0, j).start()
    for c in loads:
        c.wait()
    if zs == 0:
        mean_start()
    gathered(0)
    pump(2)

    for s in range(STEPS):
        gathered(s)
        if s > zs:
            n = s - zs - 1
            project(s, [(V.at[n], 0.5), (state_w(s).at[s], 1.0)])
            if s == 1:
                pump(8)
            y_copy(n).wait_recv()
            if s == STEPS - 1:
                mean_spread()
            hidden = (HID[...] + 0.5 * YR[n].astype(F32)) * SCALE + resb[s].astype(F32)
        else:
            project(s, [(state_w(s).at[s], 1.0)])
            hidden = HID[...] * SCALE + resb[s].astype(F32)
        HID[...] = hidden
        weighted = cotb[s].astype(F32) * gain[...]
        squares = jnp.sum(hidden * hidden, axis=0, keepdims=True)
        crosses = jnp.sum(weighted * hidden, axis=0, keepdims=True)
        SB[s, TP - 1] = jnp.concatenate(
            [v[:, 128 * a : 128 * (a + 1)] for v in (squares, crosses) for a in range(4)], axis=0
        )

        @pl.loop(1, TP)
        def _(j):
            remote(
                SB.at[s, TP - 1], SB.at[s, j - 1], sum_s.at[s], sum_r.at[s], (rep, (tp + j) % TP)
            ).start()

        pump(4)
        others = SB.at[s, pl.ds(0, TP - 1)]
        remote(others, others, sum_s.at[s], sum_r.at[s], sibling).wait_recv()
        total = jnp.sum(SB[s], axis=0)
        square_sum = jnp.concatenate([total[a : a + 1] for a in range(4)], axis=1)
        cross_sum = jnp.concatenate([total[4 + a : 5 + a] for a in range(4)], axis=1)
        inverse = lax.rsqrt(square_sum / D + EPS)
        cross_mean = cross_sum / D
        weighted = cotb[s].astype(F32) * gain[...]
        grad_hidden = (inverse * weighted - HID[...] * (inverse * inverse * inverse * cross_mean)).astype(BF)

        if s == zs:
            GH[0] = grad_hidden
            swap.start()
            if s + 1 < STEPS:
                cross_project(s + 1)
                if zs == 1:
                    mean_cross()
            else:
                mean_spread()
            swap.wait_recv()
            if zs == 2:
                remote(U, RU, u_s, u_r, peers[1]).wait_recv()

            @pl.loop(0, CH)
            def _(j):
                mine = jnp.dot(GH[0], context_block(s, j), preferred_element_type=F32)
                theirs = jnp.dot(GHQ[0], context_block(s, j, 1), preferred_element_type=F32)
                both = (mine + theirs) * (0.5 * SCALE)
                if zs == 2:
                    older = (U[j].astype(F32) + RU[j].astype(F32)) * 0.5
                    HB[s + 1, j] = (both + DECAY * older).astype(BF)
                    BB[s + 1, j] = (both * -LEARN - (LEARN * (1 + DECAY)) * older).astype(BF)
                else:
                    HB[s + 1, j] = both.astype(BF)
                    BB[s + 1, j] = (both * -LEARN).astype(BF)

            if s + 1 < STEPS:
                for j in range(CH):
                    w_copy(s + 1, j).start()
        else:
            GH2 = FM.at[s]

            @pl.loop(0, CH)
            def _(j):
                gradient = jnp.dot(grad_hidden, context_block(s, j), preferred_element_type=F32) * SCALE
                GH2[j] = (DECAY * state_m(s)[s, j].astype(F32) + gradient).astype(BF)
                fm_copy(s, j).start()

            if zs == 0 and s == 1:
                cross_project(2)
                mean_cross()
            if zs == 2 and s == 1:
                GH[1] = grad_hidden
                early.start()
            for j in range(CH):
                pump(3)
                if zs == 2 and s == 1 and j == CH - 2:
                    gathered(2)
                    mean_cross()
                w_copy(s, j).wait_recv()
                fm_copy(s, j).wait_recv()

                def rows(i, j=j):
                    fresh, theirs = FM[s, j, i].astype(F32), RM[s, j, i].astype(F32)
                    fresh_w = (state_w(s)[s, j, i].astype(F32) - LEARN * fresh).astype(BF).astype(F32)
                    their_w = (RW[s, j, i].astype(F32) - LEARN * theirs).astype(BF).astype(F32)
                    new_w = (fresh_w + their_w) * 0.5
                    new_m = (fresh + theirs) * 0.5
                    state_w(s)[s + 1, j, i] = new_w.astype(BF)
                    state_m(s)[s + 1, j, i] = new_m.astype(BF)

                by_rows(rows)
                if s + 1 < STEPS and s + 1 != zs:
                    w_copy(s + 1, j).start()
                elif not lazy:
                    pltpu.make_async_copy(WB.at[STEPS, j], w_out.at[0, :, wide(j)], outs.at[0, j]).start()
                    pltpu.make_async_copy(MB.at[STEPS, j], m_out.at[0, :, wide(j)], outs.at[1, j]).start()
            if s + 1 == ts:
                mean_start()
            if zs == 2 and s == 1:
                early.wait_recv()

                @pl.loop(0, CH)
                def _(j):
                    mine = jnp.dot(GH[1], context_block(s, j), preferred_element_type=F32)
                    theirs = jnp.dot(GHQ[1], context_block(s, j, 1), preferred_element_type=F32)
                    U[j] = ((mine + theirs) * (0.5 * SCALE)).astype(BF)

                remote(U, RU, u_s, u_r, peers[1]).start()

    if lazy:
        mean_done()
        for j in range(CH):

            def rows(i, j=j):
                WB[0, j, i] = (TM[j, 0, i].astype(F32) + BB[STEPS, j, i].astype(F32)).astype(BF)
                MB[0, j, i] = (TM[j, 1, i].astype(F32) + HB[STEPS, j, i].astype(F32)).astype(BF)

            by_rows(rows)
            pltpu.make_async_copy(WB.at[0, j], w_out.at[0, :, wide(j)], outs.at[0, j]).start()
            pltpu.make_async_copy(MB.at[0, j], m_out.at[0, :, wide(j)], outs.at[1, j]).start()
    last = 0 if lazy else STEPS
    for j in range(CH):
        pltpu.make_async_copy(WB.at[last, j], w_out.at[0, :, wide(j)], outs.at[0, j]).wait()
        pltpu.make_async_copy(MB.at[last, j], m_out.at[0, :, wide(j)], outs.at[1, j]).wait()
    for s in range(STEPS):
        sent = G.at[s, pl.ds(0, 2 * ROUNDS + far[s])]
        remote(sent, sent, ring_s.at[s], ring_r.at[s, 0, 0, 0], up).wait_send()
        sent = G.at[s, pl.ds(0, 15 + far[s])]
        remote(sent, sent, sib_s.at[s], sib_r.at[s], sibling).wait_send()
        if s != zs:
            remote(FM.at[s], RM.at[s], fm_s.at[s], fm_r.at[s, 0], peers[s]).wait_send()
            remote(RW.at[s], RW.at[s], w_s.at[s], w_r.at[s, 0], peers[s]).wait_send()
        others = SB.at[s, pl.ds(0, TP - 1)]
        remote(others, others, sum_s.at[s], sum_r.at[s], sibling).wait_send()
    if lazy:
        swap.wait_send()
        if zs == 2:
            early.wait_send()
        for n in range(after):
            y_copy(n).wait_send()
        if after != 1:
            remote(U, RU, u_s, u_r, peers[1]).wait_send()
        for m in apart:
            remote(TPB.at[quad_quarter[m]], RT.at[m], rt_s.at[m], rt_r.at[m], quad[m]).wait_send()
        for i in range(2):
            remote(TS.at[i], RTS.at[i], ts_s.at[i], ts_r.at[i], pair).wait_send()
            for m in range(3):
                tm_copy(m, i, quarter).wait_send()


def run(number, bits, operands):
    anywhere = pl.BlockSpec(memory_space=pl.ANY)
    dma = pltpu.SemaphoreType.DMA
    shard = jax.ShapeDtypeStruct((1, ROWS, HF), BF)
    chunks = (CH, ROWS, WIDE)
    lazy = 0 in bits
    many = STEPS if lazy else STEPS + 1
    scratch = [
        pltpu.VMEM((STEPS, 2 * TP, TOK, HF), BF),
        pltpu.VMEM((many, *chunks), BF),
        pltpu.VMEM((many, *chunks), BF),
        pltpu.VMEM((STEPS, *chunks), BF),
        pltpu.VMEM((STEPS, *chunks), BF),
        pltpu.VMEM((STEPS, *chunks), BF),
        pltpu.VMEM((STEPS, ROWS, SEQ), BF),
        pltpu.VMEM((STEPS, ROWS, SEQ), BF),
        pltpu.VMEM((ROWS, SEQ), F32),
        pltpu.VMEM((STEPS, TP, 8, 128), F32),
        dma((STEPS, 2, ROUNDS + 1, 2)),
        dma((STEPS,)),
        dma((STEPS,)),
        dma((STEPS,)),
        dma((2 * CH + 2 + STEPS,)),
        dma((STEPS, CH)),
        dma((STEPS,)),
        dma((STEPS, CH)),
        dma((STEPS,)),
        dma((STEPS,)),
        dma((STEPS,)),
        dma((2, CH)),
    ]
    if lazy:
        tile = (ROWS, SEQ)
        part = (2, ROWS, WIDE)
        scratch += [
            pltpu.VMEM((STEPS + 1, *chunks), BF),
            pltpu.VMEM((STEPS + 1, *chunks), BF),
            pltpu.VMEM((2, *tile), BF),
            pltpu.VMEM((2, *tile), BF),
            pltpu.VMEM((2, *chunks), BF),
            pltpu.VMEM(chunks, BF),
            pltpu.VMEM(chunks, BF),
            pltpu.VMEM((2, *tile), BF),
            pltpu.VMEM((2, *tile), BF),
            pltpu.VMEM((CH, *part), BF),
            pltpu.VMEM((3, *part), BF),
            pltpu.VMEM(part, BF),
            pltpu.VMEM(part, BF),
            pltpu.VMEM((CH, *part), BF),
            dma((2,)), dma((2,)), dma((2,)), dma((2,)), dma, dma,
            dma((3,)), dma((3,)), dma((2,)), dma((2,)), dma((3, 2)), dma((3, 2)),
        ]
    return pl.pallas_call(
        functools.partial(kernel, bits),
        out_shape=(shard, shard),
        in_specs=[anywhere] * 3 + [pl.BlockSpec(memory_space=pltpu.VMEM)] + [anywhere] * 2,
        out_specs=(anywhere, anywhere),
        scratch_shapes=scratch,
        compiler_params=pltpu.CompilerParams(
            collective_id=number, has_side_effects=True, vmem_limit_bytes=58 << 20
        ),
        name=f"window_{number}",
    )(*operands)


def on_device(context, residual, cotangent, norm_gain, weight, momentum, round_start):
    count = lax.axis_size("rep").bit_length() - 1
    gain = norm_gain.astype(F32)[:, None]
    branches = [
        functools.partial(run, first, tuple((first + s) % count for s in range(STEPS)))
        for first in range(count)
    ]
    return lax.switch(
        round_start[0] % count, [lambda *o, f=f: f(o) for f in branches],
        context, residual, cotangent, gain, weight, momentum,
    )


def solution(mesh):
    return jax.shard_map(
        on_device,
        mesh=mesh,
        in_specs=(
            P("rep", None, "tp", None),
            P("rep", None, "tp", None),
            P("rep", None, "tp", None),
            P("tp"),
            P("rep", "tp", None),
            P("rep", "tp", None),
            P(),
        ),
        out_specs=(P("rep", "tp", None), P("rep", "tp", None)),
        check_vma=False,
    )
```
